32 devices in a mesh: groups: 2 (over y), seq: 4 (over z), heads: 2 (over x), sub: 2 (over core).
Axes of the slice: x: 2, y: 2, z: 4, core: 2. Of those that a mesh axis runs over, the one named last changes fastest.
Arguments:
- queries: bfloat16 [8192, 1024], P(('groups', 'seq', 'heads'), 'sub'), parts along dimension 0, may hold values from -6 to 6
- keys: bfloat16 [8192, 1024], P(('groups', 'seq', 'heads'), 'sub'), parts along dimension 0, may hold values from -6 to 6
- values: bfloat16 [8192, 1024], P(('groups', 'seq', 'heads'), 'sub'), parts along dimension 0, may hold values from -6 to 6
- out_grad: bfloat16 [8192, 1024], P(('groups', 'seq', 'heads'), 'sub'), parts along dimension 0, may hold values from -6 to 6
- level_weights: float32 [8, 8, 8192], P('sub', None, ('groups', 'seq', 'heads')), parts along dimension 2, may hold values from 0.25 to 2
Outputs:
- grad_queries: bfloat16 [8192, 1024], P(('groups', 'seq', 'heads'), 'sub'), parts along dimension 0
- grad_keys: bfloat16 [8192, 1024], P(('groups', 'seq', 'heads'), 'sub'), parts along dimension 0
- grad_values: bfloat16 [8192, 1024], P(('groups', 'seq', 'heads'), 'sub'), parts along dimension 0
- weight_grads: float32 [8, 8, 8192], P('sub', None, ('groups', 'seq', 'heads')), parts along dimension 2
The draws below stay inside these ranges and needn't reach their ends.
There are 2 independent parts, one for each index of `groups`. The reference program is written for one: setup_inputs(seed, part) draws one part's arguments, and reference() takes and returns one part's arrays. A program takes and returns all parts, laid end to end along the dimension named above; each array names one. Nothing has to cross between parts.
All inputs are finite; a program needn't handle non-finite values.
Results may differ from the reference program's by a relative error of at most 0.0056.
Values may be sent and summed in bfloat16 or wider, within the bound.
A program may use at most 64 MiB of HBM per device.

```python
import math
import jax
import jax.numpy as jnp
from jax import lax

DH = 128
HEADS = 8
LEVELS = 8
TOK_DEV = 512
TOKENS = 4096


def level_of(own_key, extent, pieces, low, top_value):
    def one(position, parts):
        draws = jax.random.uniform(jax.random.fold_in(jax.random.fold_in(own_key, 6), position), (parts,), jnp.float32, low / len(pieces), top_value / len(pieces))
        return jnp.repeat(jnp.exp(draws), extent[position] // parts).reshape((-1,) + (1,) * (len(extent) - position - 1))

    level = one(*pieces[0])
    for cut in pieces[1:]:
        level = level * one(*cut)
    return level


def centred(own_key, shape, scale, most, shards=(), held_as=jnp.bfloat16):
    loudness = level_of(own_key, shape, shards, -0.22, 0.18) if shards else 1.0
    result = jax.random.normal(own_key, shape, jnp.float32) * scale * loudness
    return jnp.minimum(jnp.maximum(result, -most), most).astype(held_as)


def setup_inputs(seed: int = 0, part: int = 0) -> dict:
    seeds = jax.random.split(jax.random.key(seed), 6)
    part_keys = jax.random.split(jax.random.fold_in(seeds[5], part), 6)
    return {
        "queries": centred(part_keys[0], (TOKENS, HEADS * DH), 1.0, 6.0, ((0, 8), (1, 2))),
        "keys": centred(part_keys[1], (TOKENS, HEADS * DH), 1.0, 6.0, ((0, 8), (1, 2))),
        "values": centred(part_keys[2], (TOKENS, HEADS * DH), 1.0, 6.0, ((0, 8), (1, 2))),
        "out_grad": centred(part_keys[3], (TOKENS, HEADS * DH), 1.0, 6.0, ((0, 8), (1, 2))),
        "level_weights": jnp.clip(jnp.exp(math.log(2.0) - 2.0794415 * jax.random.uniform(part_keys[4], (HEADS, LEVELS, TOKENS), jnp.float32) ** level_of(part_keys[4], (HEADS, LEVELS, TOKENS), ((0, 2), (2, 8)), -0.2, 0.2)), 0.25, 2.0),
    }


def to_low(array_in):
    return lax.optimization_barrier(array_in.astype(jnp.bfloat16)).astype(jnp.float32)

def inner_block(queries_c, keys_c, values_c, grads_c, gate_zero, scale_zero):
    query_f = queries_c.astype(jnp.float32)
    key_f = keys_c.astype(jnp.float32)
    value_f = values_c.astype(jnp.float32)
    grad_f = grads_c.astype(jnp.float32)
    tok_rows = queries_c.shape[0]
    causal = jnp.tril(jnp.ones((tok_rows, tok_rows), dtype=bool))
    scores = jnp.einsum('thd,shd->hts', query_f, key_f)
    grad_dots = jnp.einsum('thd,shd->hts', grad_f, value_f)
    scores = jnp.where(causal, scores, jnp.float32(0.0))
    grad_dots = jnp.where(causal, grad_dots, jnp.float32(0.0))
    near_weight = scale_zero * lax.optimization_barrier(jnp.sum(scores * grad_dots, axis=2))
    factor = scale_zero * gate_zero[:, :, None]
    grad_mix = to_low(factor * grad_dots)
    score_mix = to_low(factor * scores)
    near_q = jnp.einsum('hts,shd->thd', grad_mix, key_f)
    near_k = jnp.einsum('hts,thd->shd', grad_mix, query_f)
    near_v = jnp.einsum('hts,thd->shd', score_mix, grad_f)
    return (near_q, near_k, near_v, near_weight)

def reference(queries, keys, values, out_grad, level_weights):
    tok_rows = TOK_DEV
    blocks_n = TOKENS // tok_rows
    head_count = HEADS
    head_width = DH
    shape_four = (blocks_n, tok_rows, head_count, head_width)
    query_h = queries.reshape(shape_four)
    key_h = keys.reshape(shape_four)
    value_h = values.reshape(shape_four)
    grad_h = out_grad.reshape(shape_four)
    gates = level_weights.astype(jnp.float32).reshape(head_count, LEVELS, blocks_n, tok_rows)
    bit_count = blocks_n.bit_length() - 1
    base_scale = 1.0 / math.sqrt(head_width * tok_rows)
    scales = [base_scale] + [base_scale / math.sqrt(2.0 ** (level_idx - 1)) for level_idx in range(1, LEVELS)]
    gate_zero = jnp.transpose(gates[:, 0], (1, 0, 2))

    def one_block(items):
        return inner_block(items[0], items[1], items[2], items[3], items[4], scales[0])
    near_q, near_k, near_v, near_weight = lax.map(one_block, (query_h, key_h, value_h, grad_h, gate_zero))
    query_f = query_h.astype(jnp.float32)
    key_f = key_h.astype(jnp.float32)
    value_f = value_h.astype(jnp.float32)
    grad_f = grad_h.astype(jnp.float32)
    key_state = jnp.einsum('cshd,cshe->chde', key_f, value_f)
    reverse_sum = jnp.zeros_like(key_state)
    grad_q = near_q
    weight_rows = [near_weight]
    for level_idx in range(1, LEVELS):
        if level_idx > bit_count:
            weight_rows.append(jnp.zeros_like(near_weight))
            continue
        half = 2 ** (level_idx - 1)
        group_n = blocks_n // (2 * half)
        split_shape = (group_n, 2, half, head_count, head_width, head_width)
        split = key_state.reshape(split_shape)
        lower = lax.optimization_barrier(jnp.sum(split[:, 0], axis=1))
        sibling = jnp.stack([jnp.zeros_like(lower), lower], axis=1)[:, :, None]
        sibling = jnp.broadcast_to(sibling, split_shape).reshape(key_state.shape)
        state_low = to_low(sibling)
        products = jnp.einsum('cthe,chde->cthd', grad_f, state_low)
        gate_now = jnp.transpose(gates[:, level_idx], (1, 2, 0))
        grad_q = grad_q + scales[level_idx] * gate_now[..., None] * products
        weight_rows.append(jnp.transpose(scales[level_idx] * lax.optimization_barrier(jnp.sum(products * query_f, axis=3)), (0, 2, 1)))
        scaled = to_low(gate_now[..., None] * query_f)
        grad_state = scales[level_idx] * jnp.einsum('cthd,cthe->chde', scaled, grad_f)
        split_grad = grad_state.reshape(split_shape)
        upper = lax.optimization_barrier(jnp.sum(split_grad[:, 1], axis=1))
        toward = jnp.stack([upper, jnp.zeros_like(upper)], axis=1)[:, :, None]
        toward = jnp.broadcast_to(toward, split_shape).reshape(key_state.shape)
        reverse_sum = reverse_sum + toward
    reverse_low = to_low(reverse_sum)
    grad_k = near_k + jnp.einsum('cshe,chde->cshd', value_f, reverse_low)
    grad_v = near_v + jnp.einsum('cshd,chde->cshe', key_f, reverse_low)
    flat = (TOKENS, head_count * head_width)
    stacked = jnp.stack(weight_rows, axis=0)
    weight_grads = jnp.transpose(stacked, (2, 0, 1, 3)).reshape(head_count, LEVELS, TOKENS)
    return (grad_q.reshape(flat).astype(jnp.bfloat16), grad_k.reshape(flat).astype(jnp.bfloat16), grad_v.reshape(flat).astype(jnp.bfloat16), weight_grads)
```

```python
import functools
import math

import jax
import jax.numpy as jnp
from jax import lax
from jax.experimental import pallas as pl
from jax.experimental.pallas import tpu as pltpu
from jax.sharding import PartitionSpec as P

F32 = jnp.float32
BF16 = jnp.bfloat16
NN = (((1,), (0,)), ((), ()))
NT = (((1,), (1,)), ((), ()))


def mm(a, b, dims=NN):
    return lax.dot_general(a, b, dims, preferred_element_type=F32)


def kernel(
    dims,
    scales,
    q_hbm,
    k_hbm,
    v_hbm,
    g_hbm,
    lw_ref,
    gq_ref,
    gk_ref,
    gv_ref,
    wg_ref,
    q_s,
    k_s,
    v_s,
    g_s,
    qt_s,
    kt_s,
    nq_s,
    nk_s,
    nv_s,
    usum_s,
    tsum_s,
    p_s,
    u_send,
    u_recv,
    t_send,
    t_recv,
    in_sem,
    us_sem,
    ur_sem,
    ts_sem,
    tr_sem,
):
    bits, fine, heads, toks, width, levels = dims
    top = bits - 1
    pos = lax.axis_index("seq") * fine + lax.axis_index("heads")
    bit_of = [(pos // (1 << b)) % 2 for b in range(bits)]
    partner = [pos + (1 - 2 * bit_of[b]) * (1 << b) for b in range(bits)]
    is_upper = [bit_of[b] == 1 for b in range(bits)]

    def where_is(b):
        return {"seq": partner[b] // fine, "heads": partner[b] % fine}

    barrier = pltpu.get_barrier_semaphore()
    for b in range(bits):
        pl.semaphore_signal(
            barrier, inc=1, device_id=where_is(b), device_id_type=pl.DeviceIdType.MESH
        )

    pairs = [(k_hbm, k_s), (v_hbm, v_s), (q_hbm, q_s), (g_hbm, g_s)]
    loads = {}
    for half in (pairs[:2], pairs[2:]):
        for h in range(heads):
            for src, dst in half:
                i = 0 if dst is k_s else 1 if dst is v_s else 2 if dst is q_s else 3
                loads[i, h] = pltpu.make_async_copy(
                    src.at[:, pl.ds(h * width, width)], dst.at[h], in_sem.at[i, h]
                )
                loads[i, h].start()

    def u_copy(b, h):
        return pltpu.make_async_remote_copy(
            src_ref=u_send.at[b, h],
            dst_ref=u_recv.at[b, h],
            send_sem=us_sem.at[b, h],
            recv_sem=ur_sem.at[b, h],
            device_id=where_is(b),
            device_id_type=pl.DeviceIdType.MESH,
        )

    def t_copy(b, h):
        return pltpu.make_async_remote_copy(
            src_ref=t_send.at[b, h],
            dst_ref=t_recv.at[b, h],
            send_sem=ts_sem.at[b, h],
            recv_sem=tr_sem.at[b, h],
            device_id=where_is(b),
            device_id_type=pl.DeviceIdType.MESH,
        )

    def u_start(b, h):
        if b < top:
            u_copy(b, h).start()
        else:
            pl.when(jnp.logical_not(is_upper[b]))(lambda: u_copy(b, h).start())

    def u_wait(b, h):
        if b < top:
            u_copy(b, h).wait()
        else:
            pl.when(jnp.logical_not(is_upper[b]))(lambda: u_copy(b, h).wait_send())
            pl.when(is_upper[b])(lambda: u_copy(b, h).wait_recv())

    def t_start(b, h):
        if b < top:
            t_copy(b, h).start()
        else:
            pl.when(is_upper[b])(lambda: t_copy(b, h).start())

    def t_wait(b, h):
        if b < top:
            t_copy(b, h).wait()
        else:
            pl.when(is_upper[b])(lambda: t_copy(b, h).wait_send())
            pl.when(jnp.logical_not(is_upper[b]))(lambda: t_copy(b, h).wait_recv())

    blank = jnp.zeros((heads, width, width), BF16)

    @pl.when(is_upper[top])
    def _():
        t_recv[top] = blank

    @pl.when(jnp.logical_not(is_upper[top]))
    def _():
        u_recv[top] = blank

    def block_state(h):
        loads[0, h].wait()
        loads[1, h].wait()
        kt = k_s[h].T
        kt_s[h] = kt
        state = mm(kt, v_s[h])
        usum_s[h] = state
        u_send[0, h] = state.astype(BF16)

    def grad_states(h):
        loads[2, h].wait()
        loads[3, h].wait()
        qt = q_s[h].T
        qt_s[h] = qt
        qt32 = qt.astype(F32)
        for level in range(bits, 0, -1):
            scaled = (lw_ref[h, level : level + 1, :] * qt32).astype(BF16)
            state = scales[level] * mm(scaled, g_s[h])
            if level == bits:
                t_send[top, h] = state.astype(BF16)
                t_start(top, h)
            else:
                p_s[level - 1, h] = state

    tile = toks // 2
    row_idx = lax.broadcasted_iota(jnp.int32, (tile, tile), 0)
    col_idx = lax.broadcasted_iota(jnp.int32, (tile, tile), 1)
    causal = row_idx <= col_idx

    def near(h):
        a, c = slice(0, tile), slice(tile, toks)
        q, k, v, g, kt = q_s[h], k_s[h], v_s[h], g_s[h], kt_s[h]
        factor = scales[0] * lw_ref[h, 0:1, :]

        def piece(rows, cols, masked):
            w = mm(k[rows], q[cols], NT)
            y = mm(v[rows], g[cols], NT)
            if masked:
                w = jnp.where(causal, w, 0.0)
                y = jnp.where(causal, y, 0.0)
            near_w = jnp.sum(w * y, axis=0, keepdims=True)
            f = factor[:, cols]
            return (f * y).astype(BF16), (f * w).astype(BF16), near_w

        gm_aa, sm_aa, nw_aa = piece(a, a, True)
        gm_ac, sm_ac, nw_ac = piece(a, c, False)
        gm_cc, sm_cc, nw_cc = piece(c, c, True)
        wg_ref[h, 0:1, a] = scales[0] * nw_aa
        wg_ref[h, 0:1, c] = scales[0] * (nw_ac + nw_cc)
        nq_s[h, :, a] = mm(kt[:, a], gm_aa)
        nq_s[h, :, c] = mm(kt[:, a], gm_ac) + mm(kt[:, c], gm_cc)
        nk_s[h, a, :] = mm(gm_aa, q[a]) + mm(gm_ac, q[c])
        nk_s[h, c, :] = mm(gm_cc, q[c])
        nv_s[h, a, :] = mm(sm_aa, g[a]) + mm(sm_ac, g[c])
        nv_s[h, c, :] = mm(sm_cc, g[c])

    def far_level(level, h):
        state = u_recv[level - 1, h]
        if level - 1 < top:
            state = jnp.where(is_upper[level - 1], state, jnp.zeros_like(state))
        products = mm(state, g_s[h], NT)
        row = jnp.sum(products * qt_s[h].astype(F32), axis=0, keepdims=True)
        wg_ref[h, level : level + 1, :] = scales[level] * row
        return (scales[level] * lw_ref[h, level : level + 1, :]) * products

    def u_round(r, h):
        u_wait(r, h)
        if r < top:
            total = usum_s[h] + u_recv[r, h].astype(F32)
            usum_s[h] = total
            u_send[r + 1, h] = total.astype(BF16)
            u_start(r + 1, h)

    def t_round(r, h):
        b = top - r
        t_wait(b, h)
        total = t_recv[b, h].astype(F32)
        if r > 0:
            total = tsum_s[h] + total
        if b > 0:
            tsum_s[h] = total
            extra = p_s[b - 1, h]
            total = total + jnp.where(is_upper[b - 1], extra, jnp.zeros_like(extra))
            t_send[b - 1, h] = total.astype(BF16)
            t_start(b - 1, h)
        return total

    for h in range(heads):
        block_state(h)
        if h == 0:
            pl.semaphore_wait(barrier, bits)
        u_start(0, h)
    for h in range(heads):
        grad_states(h)
    if bits + 1 < levels:
        wg_ref[:, bits + 1 :, :] = jnp.zeros((heads, levels - bits - 1, toks), F32)
    pending = [(level, h) for level in range(1, bits) for h in range(heads)]
    for r in range(bits):
        for h in range(heads):
            if h * bits // heads == r:
                near(h)
        for level, h in list(pending):
            if level <= r and h * bits // heads <= r:
                nq_s[h] += far_level(level, h)
                pending.remove((level, h))
        if r < top:
            for h in range(heads):
                u_round(r, h)
                t_round(r, h)
    for h in range(heads):
        cols = slice(h * width, (h + 1) * width)
        u_round(top, h)
        gq_ref[:, cols] = (nq_s[h] + far_level(bits, h)).astype(BF16).T
        low = t_round(top, h).astype(BF16)
        gk_ref[:, cols] = (nk_s[h] + mm(v_s[h], low, NT)).astype(BF16)
        gv_ref[:, cols] = (nv_s[h] + mm(k_s[h], low)).astype(BF16)


def on_device(queries, keys, values, out_grad, level_weights):
    toks, flat = queries.shape
    heads, levels = level_weights.shape[:2]
    width = flat // heads
    fine = lax.axis_size("heads")
    bits = (lax.axis_size("seq") * fine).bit_length() - 1
    base = 1.0 / math.sqrt(width * toks)
    scales = [base] + [base / math.sqrt(2.0 ** (i - 1)) for i in range(1, levels)]
    dims = (bits, fine, heads, toks, width, levels)
    hbm = pl.BlockSpec(memory_space=pltpu.MemorySpace.HBM)
    vmem = pl.BlockSpec(memory_space=pltpu.MemorySpace.VMEM)
    tok_major = pltpu.VMEM((heads, toks, width), BF16)
    feat_major = pltpu.VMEM((heads, width, toks), BF16)
    state = pltpu.VMEM((heads, width, width), F32)
    slots = pltpu.VMEM((bits, heads, width, width), BF16)
    sems = pltpu.SemaphoreType.DMA((bits, heads))
    return pl.pallas_call(
        functools.partial(kernel, dims, scales),
        out_shape=(
            jax.ShapeDtypeStruct((toks, flat), BF16),
            jax.ShapeDtypeStruct((toks, flat), BF16),
            jax.ShapeDtypeStruct((toks, flat), BF16),
            jax.ShapeDtypeStruct((heads, levels, toks), F32),
        ),
        in_specs=[hbm, hbm, hbm, hbm, vmem],
        out_specs=(vmem, vmem, vmem, vmem),
        scratch_shapes=[
            tok_major,
            tok_major,
            tok_major,
            tok_major,
            feat_major,
            feat_major,
            pltpu.VMEM((heads, width, toks), F32),
            pltpu.VMEM((heads, toks, width), F32),
            pltpu.VMEM((heads, toks, width), F32),
            state,
            state,
            pltpu.VMEM((max(bits - 1, 1), heads, width, width), F32),
            slots,
            slots,
            slots,
            slots,
            pltpu.SemaphoreType.DMA((4, heads)),
            sems,
            sems,
            sems,
            sems,
        ],
        compiler_params=pltpu.CompilerParams(
            collective_id=0, has_side_effects=True, vmem_limit_bytes=40 * 1024 * 1024
        ),
    )(queries, keys, values, out_grad, level_weights)


def solution(mesh):
    rows = P(("groups", "seq", "heads"), "sub")
    weights = P("sub", None, ("groups", "seq", "heads"))
    return jax.shard_map(
        on_device,
        mesh=mesh,
        in_specs=(rows, rows, rows, rows, weights),
        out_specs=(rows, rows, rows, weights),
        check_vma=False,
    )
```

```python
import functools
import math

import jax
import jax.numpy as jnp
from jax import lax
from jax.experimental import pallas as pl
from jax.experimental.pallas import tpu as pltpu
from jax.sharding import PartitionSpec as P

F32 = jnp.float32
BF16 = jnp.bfloat16
NN = (((1,), (0,)), ((), ()))
NT = (((1,), (1,)), ((), ()))


def mm(a, b, dims=NN):
    return lax.dot_general(a, b, dims, preferred_element_type=F32)


def kernel(
    dims,
    scales,
    q_hbm,
    k_hbm,
    v_hbm,
    g_hbm,
    lw_hbm,
    gq_ref,
    gk_ref,
    gv_ref,
    wg_ref,
    q_s,
    k_s,
    v_s,
    g_s,
    qt_s,
    kt_s,
    nq_s,
    nk_s,
    nv_s,
    usum_s,
    tsum_s,
    p_s,
    u_send,
    u_recv,
    t_send,
    t_recv,
    lw_ref,
    in_sem,
    lw_sem,
    us_sem,
    ur_sem,
    ts_sem,
    tr_sem,
):
    bits, fine, heads, toks, width, levels = dims
    top = bits - 1
    pos = lax.axis_index("seq") * fine + lax.axis_index("heads")
    bit_of = [(pos // (1 << b)) % 2 for b in range(bits)]
    partner = [pos + (1 - 2 * bit_of[b]) * (1 << b) for b in range(bits)]
    is_upper = [bit_of[b] == 1 for b in range(bits)]

    def where_is(b):
        return {"seq": partner[b] // fine, "heads": partner[b] % fine}

    barrier = pltpu.get_barrier_semaphore()
    for b in range(bits):
        pl.semaphore_signal(
            barrier, inc=1, device_id=where_is(b), device_id_type=pl.DeviceIdType.MESH
        )

    pairs = [(k_hbm, k_s), (v_hbm, v_s), (q_hbm, q_s), (g_hbm, g_s)]
    loads = {}
    for half in (pairs[:2], pairs[2:]):
        for h in range(heads):
            for src, dst in half:
                i = 0 if dst is k_s else 1 if dst is v_s else 2 if dst is q_s else 3
                loads[i, h] = pltpu.make_async_copy(
                    src.at[:, pl.ds(h * width, width)], dst.at[h], in_sem.at[i, h]
                )
                loads[i, h].start()

    lw_load = pltpu.make_async_copy(lw_hbm, lw_ref, lw_sem)
    lw_load.start()

    def u_copy(b, h):
        return pltpu.make_async_remote_copy(
            src_ref=u_send.at[b, h],
            dst_ref=u_recv.at[b, h],
            send_sem=us_sem.at[b, h],
            recv_sem=ur_sem.at[b, h],
            device_id=where_is(b),
            device_id_type=pl.DeviceIdType.MESH,
        )

    def t_copy(b, h):
        return pltpu.make_async_remote_copy(
            src_ref=t_send.at[b, h],
            dst_ref=t_recv.at[b, h],
            send_sem=ts_sem.at[b, h],
            recv_sem=tr_sem.at[b, h],
            device_id=where_is(b),
            device_id_type=pl.DeviceIdType.MESH,
        )

    def u_start(b, h):
        if b < top:
            u_copy(b, h).start()
        else:
            pl.when(jnp.logical_not(is_upper[b]))(lambda: u_copy(b, h).start())

    def u_wait(b, h):
        if b < top:
            u_copy(b, h).wait()
        else:
            pl.when(jnp.logical_not(is_upper[b]))(lambda: u_copy(b, h).wait_send())
            pl.when(is_upper[b])(lambda: u_copy(b, h).wait_recv())

    def t_start(b, h):
        if b < top:
            t_copy(b, h).start()
        else:
            pl.when(is_upper[b])(lambda: t_copy(b, h).start())

    def t_wait(b, h):
        if b < top:
            t_copy(b, h).wait()
        else:
            pl.when(is_upper[b])(lambda: t_copy(b, h).wait_send())
            pl.when(jnp.logical_not(is_upper[b]))(lambda: t_copy(b, h).wait_recv())

    blank = jnp.zeros((heads, width, width), BF16)

    @pl.when(is_upper[top])
    def _():
        t_recv[top] = blank

    @pl.when(jnp.logical_not(is_upper[top]))
    def _():
        u_recv[top] = blank

    def block_state(h):
        loads[0, h].wait()
        loads[1, h].wait()
        kt = k_s[h].T
        kt_s[h] = kt
        state = mm(kt, v_s[h])
        usum_s[h] = state
        u_send[0, h] = state.astype(BF16)

    def grad_states(h):
        loads[2, h].wait()
        loads[3, h].wait()
        qt = q_s[h].T
        qt_s[h] = qt
        qt32 = qt.astype(F32)
        for level in range(bits, 0, -1):
            scaled = (lw_ref[h, level : level + 1, :] * qt32).astype(BF16)
            state = scales[level] * mm(scaled, g_s[h])
            if level == bits:
                t_send[top, h] = state.astype(BF16)
                t_start(top, h)
            else:
                p_s[level - 1, h] = state

    tile = toks // 2
    row_idx = lax.broadcasted_iota(jnp.int32, (tile, tile), 0)
    col_idx = lax.broadcasted_iota(jnp.int32, (tile, tile), 1)
    causal = row_idx <= col_idx

    def near(h):
        a, c = slice(0, tile), slice(tile, toks)
        q, k, v, g, kt = q_s[h], k_s[h], v_s[h], g_s[h], kt_s[h]
        factor = scales[0] * lw_ref[h, 0:1, :]

        def piece(rows, cols, masked):
            w = mm(k[rows], q[cols], NT)
            y = mm(v[rows], g[cols], NT)
            if masked:
                w = jnp.where(causal, w, 0.0)
                y = jnp.where(causal, y, 0.0)
            near_w = jnp.sum(w * y, axis=0, keepdims=True)
            f = factor[:, cols]
            return (f * y).astype(BF16), (f * w).astype(BF16), near_w

        gm_aa, sm_aa, nw_aa = piece(a, a, True)
        gm_ac, sm_ac, nw_ac = piece(a, c, False)
        gm_cc, sm_cc, nw_cc = piece(c, c, True)
        wg_ref[h, 0:1, a] = scales[0] * nw_aa
        wg_ref[h, 0:1, c] = scales[0] * (nw_ac + nw_cc)
        nq_s[h, :, a] = mm(kt[:, a], gm_aa)
        nq_s[h, :, c] = mm(kt[:, a], gm_ac) + mm(kt[:, c], gm_cc)
        nk_s[h, a, :] = mm(gm_aa, q[a]) + mm(gm_ac, q[c])
        nk_s[h, c, :] = mm(gm_cc, q[c])
        nv_s[h, a, :] = mm(sm_aa, g[a]) + mm(sm_ac, g[c])
        nv_s[h, c, :] = mm(sm_cc, g[c])

    def far_level(level, h):
        state = u_recv[level - 1, h]
        if level - 1 < top:
            state = jnp.where(is_upper[level - 1], state, jnp.zeros_like(state))
        products = mm(state, g_s[h], NT)
        row = jnp.sum(products * qt_s[h].astype(F32), axis=0, keepdims=True)
        wg_ref[h, level : level + 1, :] = scales[level] * row
        return (scales[level] * lw_ref[h, level : level + 1, :]) * products

    def u_round(r, h):
        u_wait(r, h)
        if r < top:
            total = usum_s[h] + u_recv[r, h].astype(F32)
            usum_s[h] = total
            u_send[r + 1, h] = total.astype(BF16)
            u_start(r + 1, h)

    def t_round(r, h):
        b = top - r
        t_wait(b, h)
        total = t_recv[b, h].astype(F32)
        if r > 0:
            total = tsum_s[h] + total
        if b > 0:
            tsum_s[h] = total
            extra = p_s[b - 1, h]
            total = total + jnp.where(is_upper[b - 1], extra, jnp.zeros_like(extra))
            t_send[b - 1, h] = total.astype(BF16)
            t_start(b - 1, h)
        return total

    for h in range(heads):
        block_state(h)
        if h == 0:
            pl.semaphore_wait(barrier, bits)
        u_start(0, h)
    lw_load.wait()
    for h in range(heads):
        grad_states(h)
    if bits + 1 < levels:
        wg_ref[:, bits + 1 :, :] = jnp.zeros((heads, levels - bits - 1, toks), F32)
    pending = [(level, h) for level in range(1, bits) for h in range(heads)]
    for r in range(bits):
        for h in range(heads):
            if h * bits // heads == r:
                near(h)
        for level, h in list(pending):
            if level <= r and h * bits // heads <= r:
                nq_s[h] += far_level(level, h)
                pending.remove((level, h))
        if r < top:
            for h in range(heads):
                u_round(r, h)
                t_round(r, h)
    for h in range(heads):
        cols = slice(h * width, (h + 1) * width)
        u_round(top, h)
        gq_ref[:, cols] = (nq_s[h] + far_level(bits, h)).astype(BF16).T
        low = t_round(top, h).astype(BF16)
        gk_ref[:, cols] = (nk_s[h] + mm(v_s[h], low, NT)).astype(BF16)
        gv_ref[:, cols] = (nv_s[h] + mm(k_s[h], low)).astype(BF16)


def store_kernel(*refs):
    count = (len(refs) - 1) // 2
    sems = refs[-1]
    copies = [
        pltpu.make_async_copy(refs[i], refs[count + i], sems.at[i]) for i in range(count)
    ]
    for copy in copies:
        copy.start()
    for copy in copies:
        copy.wait()


def on_device(queries, keys, values, out_grad, level_weights):
    toks, flat = queries.shape
    heads, levels = level_weights.shape[:2]
    width = flat // heads
    fine = lax.axis_size("heads")
    bits = (lax.axis_size("seq") * fine).bit_length() - 1
    base = 1.0 / math.sqrt(width * toks)
    scales = [base] + [base / math.sqrt(2.0 ** (i - 1)) for i in range(1, levels)]
    dims = (bits, fine, heads, toks, width, levels)
    hbm = pl.BlockSpec(memory_space=pltpu.MemorySpace.HBM)
    vmem = pl.BlockSpec(memory_space=pltpu.MemorySpace.VMEM)
    tok_major = pltpu.VMEM((heads, toks, width), BF16)
    feat_major = pltpu.VMEM((heads, width, toks), BF16)
    state = pltpu.VMEM((heads, width, width), F32)
    slots = pltpu.VMEM((bits, heads, width, width), BF16)
    sems = pltpu.SemaphoreType.DMA((bits, heads))
    results = pl.pallas_call(
        functools.partial(kernel, dims, scales),
        out_shape=(
            pltpu.VMEM((toks, flat), BF16),
            pltpu.VMEM((toks, flat), BF16),
            pltpu.VMEM((toks, flat), BF16),
            pltpu.VMEM((heads, levels, toks), F32),
        ),
        in_specs=[hbm, hbm, hbm, hbm, hbm],
        out_specs=(vmem, vmem, vmem, vmem),
        scratch_shapes=[
            tok_major,
            tok_major,
            tok_major,
            tok_major,
            feat_major,
            feat_major,
            pltpu.VMEM((heads, width, toks), F32),
            pltpu.VMEM((heads, toks, width), F32),
            pltpu.VMEM((heads, toks, width), F32),
            state,
            state,
            pltpu.VMEM((max(bits - 1, 1), heads, width, width), F32),
            slots,
            slots,
            slots,
            slots,
            pltpu.VMEM((heads, levels, toks), F32),
            pltpu.SemaphoreType.DMA((4, heads)),
            pltpu.SemaphoreType.DMA,
            sems,
            sems,
            sems,
            sems,
        ],
        compiler_params=pltpu.CompilerParams(
            collective_id=0, has_side_effects=True, vmem_limit_bytes=60000 * 1024
        ),
    )(queries, keys, values, out_grad, level_weights)
    return pl.pallas_call(
        store_kernel,
        out_shape=tuple(jax.ShapeDtypeStruct(x.shape, x.dtype) for x in results),
        in_specs=[vmem] * len(results),
        out_specs=(hbm,) * len(results),
        scratch_shapes=[pltpu.SemaphoreType.DMA((len(results),))],
        compiler_params=pltpu.CompilerParams(vmem_limit_bytes=1024 * 1024),
    )(*results)


def solution(mesh):
    rows = P(("groups", "seq", "heads"), "sub")
    weights = P("sub", None, ("groups", "seq", "heads"))
    return jax.shard_map(
        on_device,
        mesh=mesh,
        in_specs=(rows, rows, rows, rows, weights),
        out_specs=(rows, rows, rows, weights),
        check_vma=False,
    )
```

```python
import functools
import math

import jax
import jax.numpy as jnp
from jax import lax
from jax.experimental import pallas as pl
from jax.experimental.pallas import tpu as pltpu
from jax.sharding import PartitionSpec as P

F32 = jnp.float32
BF16 = jnp.bfloat16
NN = (((1,), (0,)), ((), ()))
NT = (((1,), (1,)), ((), ()))


def mm(a, b, dims=NN):
    return lax.dot_general(a, b, dims, preferred_element_type=F32)


def kernel(
    dims,
    scales,
    q_hbm,
    k_hbm,
    v_hbm,
    g_hbm,
    lw_hbm,
    gq_ref,
    gk_ref,
    gv_ref,
    wg_ref,
    q_s,
    k_s,
    v_s,
    g_s,
    qt_s,
    kt_s,
    nq_s,
    nk_s,
    nv_s,
    usum_s,
    tsum_s,
    p_s,
    u_send,
    u_recv,
    t_send,
    t_recv,
    lw_ref,
    in_sem,
    lw_sem,
    us_sem,
    ur_sem,
    ts_sem,
    tr_sem,
):
    bits, x_bits, heads, toks, width, levels = dims
    top = bits - 1
    z_bits = bits - x_bits
    x_pos = lax.axis_index("heads")
    z_pos = lax.axis_index("seq")
    z_size = 1 << z_bits
    x_bit = [(x_pos // (1 << b)) % 2 for b in range(x_bits)]
    x_peer = [x_pos + (1 - 2 * x_bit[b]) * (1 << b) for b in range(x_bits)]
    x_upper = [x_bit[b] == 1 for b in range(x_bits)]
    has_next = z_pos < z_size - 1
    has_prev = z_pos > 0
    spot = [z_pos % (2 << c) for c in range(z_bits)]
    in_upper = [spot[c] >= (1 << c) for c in range(z_bits)]
    holds_low = [spot[c] == (1 << c) - 1 for c in range(z_bits)]
    is_last = [spot[c] == (2 << c) - 1 for c in range(z_bits)]
    not_last = [spot[c] < (2 << c) - 1 for c in range(z_bits)]
    relays = [jnp.logical_and(in_upper[c], not_last[c]) for c in range(z_bits)]
    t_takes = [jnp.logical_and(spot[c] >= (1 << c) - 1, not_last[c]) for c in range(z_bits)]

    def reach(b, step):
        if b < x_bits:
            return {"heads": x_peer[b]}
        return {"seq": z_pos + step}

    mesh_ids = pl.DeviceIdType.MESH
    barrier = pltpu.get_barrier_semaphore()
    for b in range(x_bits):
        pl.semaphore_signal(barrier, inc=1, device_id=reach(b, 0), device_id_type=mesh_ids)

    @pl.when(has_next)
    def _():
        pl.semaphore_signal(
            barrier, inc=1, device_id={"seq": z_pos + 1}, device_id_type=mesh_ids
        )

    @pl.when(has_prev)
    def _():
        pl.semaphore_signal(
            barrier, inc=1, device_id={"seq": z_pos - 1}, device_id_type=mesh_ids
        )

    def barrier_wait():
        ends = jnp.where(has_next, 1, 0) + jnp.where(has_prev, 1, 0)
        pl.semaphore_wait(barrier, x_bits + ends)

    pairs = [(k_hbm, k_s), (v_hbm, v_s), (q_hbm, q_s), (g_hbm, g_s)]
    loads = {}
    for half in (pairs[:2], pairs[2:]):
        for h in range(heads):
            for src, dst in half:
                i = 0 if dst is k_s else 1 if dst is v_s else 2 if dst is q_s else 3
                loads[i, h] = pltpu.make_async_copy(
                    src.at[:, pl.ds(h * width, width)], dst.at[h], in_sem.at[i, h]
                )
                loads[i, h].start()

    lw_load = pltpu.make_async_copy(lw_hbm, lw_ref, lw_sem)
    lw_load.start()

    def u_copy(b, h, source=None):
        return pltpu.make_async_remote_copy(
            src_ref=(u_send if source is None else source).at[b, h],
            dst_ref=u_recv.at[b, h],
            send_sem=us_sem.at[b, h],
            recv_sem=ur_sem.at[b, h],
            device_id=reach(b, 1),
            device_id_type=mesh_ids,
        )

    def t_copy(b, h):
        return pltpu.make_async_remote_copy(
            src_ref=t_send.at[b, h],
            dst_ref=t_recv.at[b, h],
            send_sem=ts_sem.at[b, h],
            recv_sem=tr_sem.at[b, h],
            device_id=reach(b, -1),
            device_id_type=mesh_ids,
        )

    blank = jnp.zeros((heads, width, width), BF16)
    for c in range(z_bits):

        @pl.when(jnp.logical_not(in_upper[c]))
        def _():
            u_recv[x_bits + c] = blank

        @pl.when(jnp.logical_not(t_takes[c]))
        def _():
            t_recv[x_bits + c] = blank

    def block_state(h):
        loads[0, h].wait()
        loads[1, h].wait()
        kt = k_s[h].T
        kt_s[h] = kt
        state = mm(kt, v_s[h])
        usum_s[h] = state
        u_send[0, h] = state.astype(BF16)

    def grad_states(h):
        loads[2, h].wait()
        loads[3, h].wait()
        qt = q_s[h].T
        qt_s[h] = qt
        qt32 = qt.astype(F32)
        for level in range(bits, 0, -1):
            scaled = (lw_ref[h, level : level + 1, :] * qt32).astype(BF16)
            state = scales[level] * mm(scaled, g_s[h])
            p_s[level - 1, h] = state
            if level == bits:
                tsum_s[h] = jnp.zeros((width, width), F32)
                t_first(z_bits - 1, h)

    tile = toks // 2
    row_idx = lax.broadcasted_iota(jnp.int32, (tile, tile), 0)
    col_idx = lax.broadcasted_iota(jnp.int32, (tile, tile), 1)
    causal = row_idx <= col_idx

    def near(h):
        a, c = slice(0, tile), slice(tile, toks)
        q, k, v, g, kt = q_s[h], k_s[h], v_s[h], g_s[h], kt_s[h]
        factor = scales[0] * lw_ref[h, 0:1, :]

        def piece(rows, cols, masked):
            w = mm(k[rows], q[cols], NT)
            y = mm(v[rows], g[cols], NT)
            if masked:
                w = jnp.where(causal, w, 0.0)
                y = jnp.where(causal, y, 0.0)
            near_w = jnp.sum(w * y, axis=0, keepdims=True)
            f = factor[:, cols]
            return (f * y).astype(BF16), (f * w).astype(BF16), near_w

        gm_aa, sm_aa, nw_aa = piece(a, a, True)
        gm_ac, sm_ac, nw_ac = piece(a, c, False)
        gm_cc, sm_cc, nw_cc = piece(c, c, True)
        wg_ref[h, 0:1, a] = scales[0] * nw_aa
        wg_ref[h, 0:1, c] = scales[0] * (nw_ac + nw_cc)
        nq_s[h, :, a] = mm(kt[:, a], gm_aa)
        nq_s[h, :, c] = mm(kt[:, a], gm_ac) + mm(kt[:, c], gm_cc)
        nk_s[h, a, :] = mm(gm_aa, q[a]) + mm(gm_ac, q[c])
        nk_s[h, c, :] = mm(gm_cc, q[c])
        nv_s[h, a, :] = mm(sm_aa, g[a]) + mm(sm_ac, g[c])
        nv_s[h, c, :] = mm(sm_cc, g[c])

    def far_level(level, h):
        state = u_recv[level - 1, h]
        if level - 1 < x_bits:
            state = jnp.where(x_upper[level - 1], state, jnp.zeros_like(state))
        products = mm(state, g_s[h], NT)
        row = jnp.sum(products * qt_s[h].astype(F32), axis=0, keepdims=True)
        wg_ref[h, level : level + 1, :] = scales[level] * row
        return (scales[level] * lw_ref[h, level : level + 1, :]) * products

    def u_next(b, h, total):
        if b > top:
            return
        u_send[b, h] = total.astype(BF16)
        if b < x_bits:
            u_copy(b, h).start()
        else:
            pl.when(holds_low[b - x_bits])(lambda: u_copy(b, h).start())

    def u_round(b, h):
        if b < x_bits:
            u_copy(b, h).wait()
            total = usum_s[h] + u_recv[b, h].astype(F32)
        else:
            c = b - x_bits
            pl.when(in_upper[c])(lambda: u_copy(b, h).wait_recv())
            pl.when(relays[c])(lambda: u_copy(b, h, u_recv).start())
            if b == top:
                return
            total = usum_s[h] + u_recv[b, h].astype(F32)
        usum_s[h] = total
        u_next(b + 1, h, total)

    def t_first(c, h):
        b = x_bits + c

        @pl.when(is_last[c])
        def _():
            t_send[b, h] = (tsum_s[h] + p_s[b, h]).astype(BF16)
            t_copy(b, h).start()

    def t_round(r, h):
        b = top - r
        if b < x_bits:
            t_copy(b, h).wait()
            total = tsum_s[h] + t_recv[b, h].astype(F32)
        else:
            c = b - x_bits
            pl.when(t_takes[c])(lambda: t_copy(b, h).wait_recv())

            @pl.when(relays[c])
            def _():
                t_send[b, h] = (t_recv[b, h].astype(F32) + p_s[b, h]).astype(BF16)
                t_copy(b, h).start()

            got = t_recv[b, h].astype(F32)
            total = tsum_s[h] + jnp.where(holds_low[c], got, jnp.zeros_like(got))
        if b == 0:
            return total
        tsum_s[h] = total
        if b > x_bits:
            t_first(b - 1 - x_bits, h)
        else:
            extra = p_s[b - 1, h]
            extra = jnp.where(x_upper[b - 1], extra, jnp.zeros_like(extra))
            t_send[b - 1, h] = (total + extra).astype(BF16)
            t_copy(b - 1, h).start()

    for h in range(heads):
        block_state(h)
        if h == 0:
            barrier_wait()
        u_copy(0, h).start()
    lw_load.wait()
    for h in range(heads):
        grad_states(h)
    if bits + 1 < levels:
        wg_ref[:, bits + 1 :, :] = jnp.zeros((heads, levels - bits - 1, toks), F32)
    pending = [(level, h) for level in range(1, bits) for h in range(heads)]
    for r in range(bits):
        for h in range(heads):
            if h * bits // heads == r:
                near(h)
        for level, h in list(pending):
            if level <= r and h * bits // heads <= r:
                nq_s[h] += far_level(level, h)
                pending.remove((level, h))
        for h in range(heads):
            if r > 0:
                t_round(r - 1, h)
            u_round(r, h)
            if r == top:
                cols = slice(h * width, (h + 1) * width)
                gq_ref[:, cols] = (nq_s[h] + far_level(bits, h)).astype(BF16).T
    for h in range(heads):
        cols = slice(h * width, (h + 1) * width)
        low = t_round(top, h).astype(BF16)
        gk_ref[:, cols] = (nk_s[h] + mm(v_s[h], low, NT)).astype(BF16)
        gv_ref[:, cols] = (nv_s[h] + mm(k_s[h], low)).astype(BF16)
    for c in range(z_bits):
        sends = jnp.logical_or(holds_low[c], relays[c])
        for h in range(heads):
            b = x_bits + c
            pl.when(sends)(lambda: u_copy(b, h).wait_send())
            pl.when(in_upper[c])(lambda: t_copy(b, h).wait_send())


def store_kernel(*refs):
    count = (len(refs) - 1) // 2
    sems = refs[-1]
    copies = [
        pltpu.make_async_copy(refs[i], refs[count + i], sems.at[i]) for i in range(count)
    ]
    for copy in copies:
        copy.start()
    for copy in copies:
        copy.wait()


def on_device(queries, keys, values, out_grad, level_weights):
    toks, flat = queries.shape
    heads, levels = level_weights.shape[:2]
    width = flat // heads
    fine = lax.axis_size("heads")
    bits = (lax.axis_size("seq") * fine).bit_length() - 1
    base = 1.0 / math.sqrt(width * toks)
    scales = [base] + [base / math.sqrt(2.0 ** (i - 1)) for i in range(1, levels)]
    dims = (bits, fine.bit_length() - 1, heads, toks, width, levels)
    hbm = pl.BlockSpec(memory_space=pltpu.MemorySpace.HBM)
    vmem = pl.BlockSpec(memory_space=pltpu.MemorySpace.VMEM)
    tok_major = pltpu.VMEM((heads, toks, width), BF16)
    feat_major = pltpu.VMEM((heads, width, toks), BF16)
    state = pltpu.VMEM((heads, width, width), F32)
    slots = pltpu.VMEM((bits, heads, width, width), BF16)
    sems = pltpu.SemaphoreType.DMA((bits, heads))
    results = pl.pallas_call(
        functools.partial(kernel, dims, scales),
        out_shape=(
            pltpu.VMEM((toks, flat), BF16),
            pltpu.VMEM((toks, flat), BF16),
            pltpu.VMEM((toks, flat), BF16),
            pltpu.VMEM((heads, levels, toks), F32),
        ),
        in_specs=[hbm, hbm, hbm, hbm, hbm],
        out_specs=(vmem, vmem, vmem, vmem),
        scratch_shapes=[
            tok_major,
            tok_major,
            tok_major,
            tok_major,
            feat_major,
            feat_major,
            pltpu.VMEM((heads, width, toks), F32),
            pltpu.VMEM((heads, toks, width), F32),
            pltpu.VMEM((heads, toks, width), F32),
            state,
            state,
            pltpu.VMEM((bits, heads, width, width), F32),
            slots,
            slots,
            slots,
            slots,
            pltpu.VMEM((heads, levels, toks), F32),
            pltpu.SemaphoreType.DMA((4, heads)),
            pltpu.SemaphoreType.DMA,
            sems,
            sems,
            sems,
            sems,
        ],
        compiler_params=pltpu.CompilerParams(
            collective_id=0, has_side_effects=True, vmem_limit_bytes=60000 * 1024
        ),
    )(queries, keys, values, out_grad, level_weights)
    return pl.pallas_call(
        store_kernel,
        out_shape=tuple(jax.ShapeDtypeStruct(x.shape, x.dtype) for x in results),
        in_specs=[vmem] * len(results),
        out_specs=(hbm,) * len(results),
        scratch_shapes=[pltpu.SemaphoreType.DMA((len(results),))],
        compiler_params=pltpu.CompilerParams(vmem_limit_bytes=1024 * 1024),
    )(*results)


def solution(mesh):
    rows = P(("groups", "seq", "heads"), "sub")
    weights = P("sub", None, ("groups", "seq", "heads"))
    return jax.shard_map(
        on_device,
        mesh=mesh,
        in_specs=(rows, rows, rows, rows, weights),
        out_specs=(rows, rows, rows, weights),
        check_vma=False,
    )
```
